32 devices in a mesh: req: 4 (over z), tok: 8 (over y, x, core).
Axes of the slice: x: 2, y: 2, z: 4, core: 2. Of those that a mesh axis runs over, the one named last changes fastest.
Arguments:
- hidden_in: bfloat16 [4096, 2048], P(('req', 'tok')), may hold values from -1.5 to 1.5
- suffix_len: int32 [4, 4], P('req'), may hold values from 1 to 512, 1024 in all within a row
- prefix_of: int32 [4, 4], P('req'), may hold values from 0 to 3
- prefix_slot: int32 [4], replicated, may hold values from 0 to 3, each once
- prefix_cache: bfloat16 [4, 4, 2048, 128], P('req', None, 'tok'), may hold values from -160 to 160
- attn_gain: bfloat16 [2048], replicated, may hold values from 0.099609375 to 1.8984375
- query_weight: bfloat16 [2048, 2048], P(None, 'tok'), may hold values from -0.125 to 0.125
- keyval_weight: bfloat16 [4, 2048, 128], replicated, may hold values from -0.125 to 0.125
- out_weight: bfloat16 [2048, 2048], P('tok'), may hold values from -0.125 to 0.125
- mlp_gain: bfloat16 [2048], replicated, may hold values from 0.099609375 to 1.8984375
- gate_weight: bfloat16 [2048, 4096], P(None, 'req'), may hold values from -0.125 to 0.125
- up_weight: bfloat16 [2048, 4096], P(None, 'req'), may hold values from -0.125 to 0.125
- down_weight: bfloat16 [4096, 2048], P('req'), may hold values from -0.09375 to 0.09375
- final_gain: bfloat16 [2048], replicated, may hold values from 0.099609375 to 1.8984375
- head_weight: bfloat16 [32000, 2048], P('tok'), may hold values from -7 to 7
Outputs:
- hidden_out: bfloat16 [4096, 2048], P(('req', 'tok'))
- suffix_cache: bfloat16 [4096, 512], P('req', 'tok')
- last_rms: float32 [4, 4], P('req')
- top_logit: float32 [4, 4], P('req')
- log_total: float32 [4, 4], P('req')
The draws below stay inside these ranges and needn't reach their ends.
Inputs may be any that keep to these rules, and one draw needn't show every extreme that they name: `suffix_len`: each owner's 4 lengths sum to 1024, and the largest of each owner is 512.
All inputs are finite; a program needn't handle non-finite values.
Results may differ from the reference program's by a relative error of at most 0.02.
Values may be sent and summed in bfloat16 or wider, within the bound.
A program may use at most 128 MiB of HBM per device.

```python
import math
import jax
import jax.numpy as jnp
import numpy as np
from jax import lax

D = 2048
HEADS = 32
KVH = 4
HD = 64
FF = 4096
VOCAB = 32000
WINDOW = 2048
PRE_LEN = 16384
REQ_DEV = 4
OWNERS = 4
PREFIXES = 4
OWN_TOK = 1024
TOKENS = 4096
MOST = 512


def draw_prefix_cache(key, part):
    entry_key = jax.random.fold_in(key, 0)
    shape_all = (PREFIXES, KVH, WINDOW, 2 * HD)
    drawn = jnp.clip(jax.random.normal(entry_key, shape_all, jnp.float32), -4.0, 4.0)
    return drawn.astype(jnp.bfloat16)


def draw_head_weight(key, part):
    row_key, entry_key = jax.random.split(key)
    vocab_rows = jnp.arange(VOCAB)
    trend = 3.0 - 2.0 * vocab_rows.astype(jnp.float32) / VOCAB
    rough = jnp.exp(jax.random.uniform(row_key, (VOCAB, 1), jnp.float32, -1.15, 1.15))
    row_scale = 1.0 / math.sqrt(D) * trend[:, None] * rough
    drawn = jnp.clip(jax.random.normal(entry_key, (VOCAB, D), jnp.float32), -4.0, 4.0) * row_scale
    return jnp.clip(drawn, -7.0, 7.0).astype(jnp.bfloat16)


def set_ends(result, stream_key, smallest, top_value):
    spot = [jax.random.randint(jax.random.fold_in(stream_key, axis), (), 0, length) for axis, length in enumerate(result.shape)]
    main_axis = result.shape.index(max(result.shape))
    neighbour = spot[:main_axis] + [(spot[main_axis] + 1) % result.shape[main_axis]] + spot[main_axis + 1:]
    return result.at[tuple(spot)].set(smallest).at[tuple(neighbour)].set(top_value)


def level_of(rng, shape, shards, least, top_value):
    gain = 1.0
    for dim, parts in shards:
        steps = jax.random.uniform(jax.random.fold_in(jax.random.fold_in(rng, 6), dim), (parts,), jnp.float32, least / len(shards), top_value / len(shards))
        gain = gain * jnp.repeat(jnp.exp(steps), shape[dim] // parts).reshape((-1,) + (1,) * (len(shape) - 1 - dim))
    return gain


def rank_bounds(number_of, slope):
    weights = [(1 << 20) // math.isqrt(grade ** slope) + 1 for grade in range(1, number_of + 1)]
    scale = 1 + sum(weights) // (1 << 30)
    return np.cumsum(np.array([max(1, weight // scale) for weight in weights]))


def ranked_ids(own_key, extent, count, lean):
    table = rank_bounds(count, lean)
    ticket = jax.random.randint(jax.random.fold_in(own_key, 1), extent, 0, int(table[count - 1]))
    rank = jnp.searchsorted(jnp.asarray(table, jnp.int32), ticket, side="right")
    return jax.random.permutation(jax.random.fold_in(own_key, 2), count)[rank].astype(jnp.int32)


def profile(amount, total, limit, lean):
    loads = [(1 << 20) // math.isqrt(standing ** lean) + 1 for standing in range(2, amount + 1)]
    spare, holding = total - limit - (amount - 1), [1] * (amount - 1)
    while spare > 0:
        movable = [i for i in range(amount - 1) if holding[i] < limit]
        mass, left = sum([loads[i] for i in movable]), spare
        for i in movable:
            addition = min(limit - holding[i], max(1, left * loads[i] // mass), spare)
            holding[i] = holding[i] + addition
            spare = spare - addition
    return np.array([limit] + holding)


def ragged(stream_key, count, total, limit, slope):
    if count == 2:
        one = jax.random.randint(stream_key, (), max(1, total - limit), min(limit, total - 1) + 1)
        return jnp.stack([one, total - one])
    tallies = jnp.asarray(profile(count, total, limit, slope), jnp.int32)
    couples = (count - 1) // 2
    source_of, receiver = tallies[1:1 + 2 * couples:2], tallies[2:2 + 2 * couples:2]
    margin = jnp.minimum(source_of - 1, limit - receiver)
    moved = jax.random.randint(jax.random.fold_in(stream_key, 1), (couples,), 0, 1 << 20) % (margin + 1)
    tallies = tallies.at[1:1 + 2 * couples:2].set(source_of - moved).at[2:2 + 2 * couples:2].set(receiver + moved)
    return tallies[jax.random.permutation(jax.random.fold_in(stream_key, 2), count)]


def centred(rng, shape, scale, limit, shards=(), kind=jnp.bfloat16):
    level = level_of(rng, shape, shards, -0.22, 0.18) if shards else 1.0
    values = jax.random.normal(rng, shape, jnp.float32) * scale * level
    return jnp.minimum(jnp.maximum(values, -limit), limit).astype(kind)


def setup_inputs(seed: int = 0) -> dict:
    keys = jax.random.split(jax.random.key(seed), 16)
    hidden_in = centred(keys[0], (TOKENS, D), 0.25, 1.5, ((0, 32),))
    suffix_len = jax.vmap(lambda own: ragged(own, REQ_DEV, OWN_TOK, MOST, 2))(jax.random.split(keys[1], OWNERS)).reshape((OWNERS, REQ_DEV)).astype(jnp.int32)
    prefix_of = set_ends(ranked_ids(keys[2], (OWNERS, REQ_DEV), PREFIXES, 2), jax.random.fold_in(keys[2], 3), 0, PREFIXES - 1).astype(jnp.int32)
    prefix_slot = jax.random.permutation(keys[3], PREFIXES).astype(jnp.int32)
    prefix_cache = draw_prefix_cache(jax.random.fold_in(keys[15], 71), 0)
    attn_gain = jnp.clip(1.0 + 0.18 * jax.random.normal(keys[5], (D,), jnp.float32), 0.099609375, 1.8984375).astype(jnp.bfloat16)
    query_weight = centred(keys[6], (D, HEADS * HD), D ** -0.5, 0.125, ((1, 8),))
    keyval_weight = centred(keys[7], (KVH, D, 2 * HD), D ** -0.5, 0.125)
    out_weight = centred(keys[8], (HEADS * HD, D), (HEADS * HD) ** -0.5, 0.125, ((0, 8),))
    mlp_gain = jnp.clip(1.0 + 0.18 * jax.random.normal(keys[9], (D,), jnp.float32), 0.099609375, 1.8984375).astype(jnp.bfloat16)
    gate_weight = centred(keys[10], (D, FF), D ** -0.5, 0.125, ((1, 4),))
    up_weight = centred(keys[11], (D, FF), D ** -0.5, 0.125, ((1, 4),))
    down_weight = centred(keys[12], (FF, D), FF ** -0.5, 0.09375, ((0, 4),))
    final_gain = jnp.clip(1.0 + 0.18 * jax.random.normal(keys[13], (D,), jnp.float32), 0.099609375, 1.8984375).astype(jnp.bfloat16)
    head_weight = draw_head_weight(jax.random.fold_in(keys[15], 71), 0)
    return dict(hidden_in=hidden_in, suffix_len=suffix_len, prefix_of=prefix_of, prefix_slot=prefix_slot, prefix_cache=prefix_cache, attn_gain=attn_gain, query_weight=query_weight, keyval_weight=keyval_weight, out_weight=out_weight, mlp_gain=mlp_gain, gate_weight=gate_weight, up_weight=up_weight, down_weight=down_weight, final_gain=final_gain, head_weight=head_weight)


epsilon = 1e-05
neg_large = -1e+30

def rms_scale(values, gain_vec):
    widened = values.astype(jnp.float32)
    mean_square = lax.optimization_barrier(jnp.mean(widened * widened, axis=-1, keepdims=True))
    return widened * lax.rsqrt(mean_square + epsilon) * gain_vec.astype(jnp.float32)

def rotate(vectors, positions):
    half_width = vectors.shape[-1] // 2
    levels = jnp.arange(half_width).astype(jnp.float32)
    inverse = jnp.exp(levels * (-2.0 * math.log(10000.0) / vectors.shape[-1]))
    angles = positions.astype(jnp.float32)[:, None] * inverse[None, :]
    cosine = jnp.cos(angles)[:, None, :]
    sine_part = jnp.sin(angles)[:, None, :]
    first_half = vectors[..., :half_width]
    second_half = vectors[..., half_width:]
    return jnp.concatenate([first_half * cosine - second_half * sine_part, second_half * cosine + first_half * sine_part], axis=-1)

def owner_layout(lengths, row_count):
    lengths = lengths.astype(jnp.int32)
    end_rows = jnp.cumsum(lengths).astype(jnp.int32)
    starts = (end_rows - lengths).astype(jnp.int32)
    row_index = jnp.arange(row_count).astype(jnp.int32)
    member = (row_index[:, None] >= starts[None, :]) & (row_index[:, None] < end_rows[None, :])
    offsets = (row_index - lax.optimization_barrier(jnp.sum(jnp.where(member, starts[None, :], 0), axis=1))).astype(jnp.int32)
    return (starts, end_rows, offsets)

def slot_lookup(chosen, prefix_slot):
    table_index = jnp.arange(prefix_slot.shape[0]).astype(jnp.int32)
    hits = chosen.astype(jnp.int32)[:, None] == table_index[None, :]
    return lax.optimization_barrier(jnp.sum(jnp.where(hits, prefix_slot.astype(jnp.int32)[None, :], 0), axis=1)).astype(jnp.int32)

def request_attention(query_block, suffix_block, window, live_len):
    row_count = query_block.shape[0]
    head_width = query_block.shape[-1]
    window_len = window.shape[1]
    suffix_major = jnp.transpose(suffix_block, (1, 0, 2))
    key_rows = jnp.concatenate([window[:, :, :head_width], suffix_major[:, :, :head_width]], axis=1)
    value_rows = jnp.concatenate([window[:, :, head_width:], suffix_major[:, :, head_width:]], axis=1)
    scores = jnp.einsum('rgke,gse->gkrs', query_block.astype(jnp.float32), key_rows.astype(jnp.float32)) * head_width ** (-0.5)
    row_index = jnp.arange(row_count).astype(jnp.int32)
    prefix_seen = jnp.arange(window_len).astype(jnp.int32)[None, :] > row_index[:, None]
    suffix_seen = (row_index[None, :] <= row_index[:, None]) & (row_index[:, None] - row_index[None, :] < window_len) & (row_index[None, :] < live_len)
    visible = jnp.concatenate([prefix_seen, suffix_seen], axis=1)
    masked = jnp.where(visible, scores, neg_large)
    highest = lax.optimization_barrier(jnp.max(masked, axis=-1, keepdims=True))
    weights = jnp.where(visible, jnp.exp(masked - highest), 0.0)
    totals = lax.optimization_barrier(jnp.sum(weights, axis=-1, keepdims=True))
    totals = jnp.where(row_index[:, None] < live_len, totals, 1.0)
    rounded = lax.optimization_barrier(weights.astype(jnp.bfloat16))
    mixed_rows = jnp.einsum('gkrs,gse->rgke', rounded.astype(jnp.float32), value_rows.astype(jnp.float32))
    mixed_rows = mixed_rows / jnp.transpose(totals, (2, 0, 1, 3))
    return mixed_rows.reshape(row_count, -1).astype(jnp.bfloat16)

def reference(hidden_in, suffix_len, prefix_of, prefix_slot, prefix_cache, attn_gain, query_weight, keyval_weight, out_weight, mlp_gain, gate_weight, up_weight, down_weight, final_gain, head_weight):
    owners = suffix_len.shape[0]
    own_rows = hidden_in.shape[0] // owners
    most_rows = own_rows // 2
    heads_per_kv = HEADS // KVH

    def one_owner(packed):
        inputs, lengths, chosen = packed
        lengths = lengths.astype(jnp.int32)
        starts, end_rows, offsets = owner_layout(lengths, own_rows)
        positions = offsets + PRE_LEN
        normed = rms_scale(inputs, attn_gain).astype(jnp.bfloat16)
        queries = jnp.dot(normed, query_weight, preferred_element_type=jnp.float32).reshape(own_rows, HEADS, HD)
        queries = rotate(queries, positions).astype(jnp.bfloat16)
        keyvals = jnp.einsum('td,gde->tge', normed.astype(jnp.float32), keyval_weight.astype(jnp.float32))
        rotated = rotate(keyvals[:, :, :HD], positions)
        keyvals = jnp.concatenate([rotated, keyvals[:, :, HD:]], axis=-1).astype(jnp.bfloat16)
        padded_queries = jnp.concatenate([queries, jnp.zeros((most_rows, HEADS, HD), jnp.bfloat16)], axis=0)
        padded_keyvals = jnp.concatenate([keyvals, jnp.zeros((most_rows, KVH, 2 * HD), jnp.bfloat16)], axis=0)
        cache_rows = slot_lookup(chosen, prefix_slot)

        def one_request(buffer, request):
            first_row, live_len, cache_row = request
            query_block = lax.dynamic_slice_in_dim(padded_queries, first_row, most_rows, 0).reshape(most_rows, KVH, heads_per_kv, HD)
            suffix_block = lax.dynamic_slice_in_dim(padded_keyvals, first_row, most_rows, 0)
            window = lax.dynamic_index_in_dim(prefix_cache, cache_row, 0, keepdims=False)
            mixed_rows = request_attention(query_block, suffix_block, window, live_len)
            current = lax.dynamic_slice_in_dim(buffer, first_row, most_rows, 0)
            keep_rows = jnp.arange(most_rows).astype(jnp.int32)[:, None] < live_len
            return (lax.dynamic_update_slice_in_dim(buffer, jnp.where(keep_rows, mixed_rows, current), first_row, 0), None)
        buffer = jnp.zeros((own_rows + most_rows, HEADS * HD), jnp.bfloat16)
        buffer, unused = lax.scan(one_request, buffer, (starts, lengths, cache_rows))
        attended = buffer[:own_rows]
        middle = (inputs.astype(jnp.float32) + jnp.dot(attended, out_weight, preferred_element_type=jnp.float32)).astype(jnp.bfloat16)
        mlp_in = rms_scale(middle, mlp_gain).astype(jnp.bfloat16)
        gate_proj = jnp.dot(mlp_in, gate_weight, preferred_element_type=jnp.float32)
        lifted = jnp.dot(mlp_in, up_weight, preferred_element_type=jnp.float32)
        hidden_act = (jax.nn.silu(gate_proj) * lifted).astype(jnp.bfloat16)
        final_state = (middle.astype(jnp.float32) + jnp.dot(hidden_act, down_weight, preferred_element_type=jnp.float32)).astype(jnp.bfloat16)
        last_rows = final_state[end_rows - 1].astype(jnp.float32)
        mean_square = lax.optimization_barrier(jnp.mean(last_rows * last_rows, axis=-1, keepdims=True))
        spread = jnp.sqrt(mean_square + epsilon)
        final_normed = (last_rows * lax.rsqrt(mean_square + epsilon) * final_gain.astype(jnp.float32)).astype(jnp.bfloat16)
        logits = lax.dot_general(final_normed, head_weight, (((1,), (1,)), ((), ())), preferred_element_type=jnp.float32)
        highest = lax.optimization_barrier(jnp.max(logits, axis=-1))
        log_total = highest + jnp.log(lax.optimization_barrier(jnp.sum(jnp.exp(logits - highest[:, None]), axis=-1)))
        return (final_state, keyvals.reshape(own_rows, KVH * 2 * HD), spread[:, 0], highest, log_total)
    results = lax.map(one_owner, (hidden_in.reshape(owners, own_rows, hidden_in.shape[1]), suffix_len, prefix_of))
    hidden_out = results[0].reshape(owners * own_rows, hidden_in.shape[1])
    suffix_cache = results[1].reshape(owners * own_rows, KVH * 2 * HD)
    return (hidden_out, suffix_cache, results[2], results[3], results[4])
```

```python
import math

import jax
import jax.numpy as jnp
from jax import lax
from jax.experimental import pallas as pl
from jax.experimental.pallas import tpu as pltpu
from jax.sharding import PartitionSpec as P

HD = 64
PRE_LEN = 16384


epsilon = 1e-05
neg_large = -1e30


def rms_scale(values, gain_vec):
    widened = values.astype(jnp.float32)
    mean_square = jnp.mean(widened * widened, axis=-1, keepdims=True)
    return widened * lax.rsqrt(mean_square + epsilon) * gain_vec.astype(jnp.float32)


def owner_layout(lengths, row_count):
    end_rows = jnp.cumsum(lengths)
    starts = end_rows - lengths
    row_index = jnp.arange(row_count)
    member = (row_index[:, None] >= starts[None, :]) & (row_index[:, None] < end_rows[None, :])
    offsets = row_index - jnp.sum(jnp.where(member, starts[None, :], 0), axis=1)
    return (starts, end_rows, offsets)


def slot_lookup(chosen, prefix_slot):
    table_index = jnp.arange(prefix_slot.shape[0])
    hits = chosen[:, None] == table_index[None, :]
    return jnp.sum(jnp.where(hits, prefix_slot[None, :], 0), axis=1)


def attention_kernel(
    member_count,
    heads,
    piece,
    most_rows,
    window_len,
    chunk,
    suffix_chunk,
    scalars,
    q_ref,
    cos_ref,
    sin_ref,
    *refs,
):
    windows = refs[:member_count]
    suffix_ref, out_ref, query_scr, high_scr, total_scr, acc_scr, result_scr = refs[member_count:]
    requests = 4
    rows = q_ref.shape[1]
    half = HD // 2
    width = heads * rows
    member = scalars[3 * requests]
    tile = pl.program_id(0)
    first_row = (tile * member_count + member) * rows
    cosine = cos_ref[...]
    sine = sin_ref[...]
    for head in range(heads):
        low = q_ref[head * HD : head * HD + half, :]
        high = q_ref[head * HD + half : (head + 1) * HD, :]
        cols = pl.ds(head * rows, rows)
        turned = jnp.concatenate(
            [
                low * cosine - high * sine,
                high * cosine + low * sine,
                jnp.zeros((HD, rows), jnp.float32),
            ],
            axis=0,
        )
        query_scr[:, cols] = (turned * (HD**-0.5 * math.log2(math.e))).astype(jnp.bfloat16)

    def absorb(keyvals, row_of_key, visible_fn):
        scores = jnp.dot(keyvals, query_scr[...], preferred_element_type=jnp.float32)
        if visible_fn is not None:
            scores = jnp.where(visible_fn(scores.shape), scores, neg_large)
        before = high_scr[...]
        after = jnp.maximum(before, jnp.max(scores, axis=0, keepdims=True))
        weights = jnp.exp2(scores - after)
        fade = jnp.exp2(before - after)
        total_scr[...] = total_scr[...] * fade + jnp.sum(weights, axis=0, keepdims=True)
        mixed = lax.dot_general(
            keyvals,
            weights.astype(jnp.bfloat16),
            (((0,), (0,)), ((), ())),
            preferred_element_type=jnp.float32,
        )
        acc_scr[...] = acc_scr[...] * fade + mixed[HD:, :]
        high_scr[...] = after

    lane_row = first_row + lax.broadcasted_iota(jnp.int32, (1, width), 1) % rows

    def one_request(request, carry):
        start = scalars[request]
        end = scalars[requests + request]
        slot = scalars[2 * requests + request]

        @pl.when((start < first_row + rows) & (end > first_row))
        def _():
            high_scr[...] = jnp.full(high_scr.shape, neg_large, jnp.float32)
            total_scr[...] = jnp.zeros(total_scr.shape, jnp.float32)
            acc_scr[...] = jnp.zeros(acc_scr.shape, jnp.float32)
            offset = lane_row - start
            local_len = windows[0].shape[1]
            for first in reversed(range(0, local_len, chunk)):
                for shift in range(member_count):
                    part = lax.rem(member + shift, member_count)

                    def prefix_seen(shape, first=first, part=part):
                        index = first + lax.broadcasted_iota(jnp.int32, (shape[0], 1), 0)
                        position = (index // piece * member_count + part) * piece + index % piece
                        return position > offset

                    masked = first // piece * member_count * piece < most_rows
                    absorb(
                        windows[shift][slot, first : first + chunk, :],
                        None,
                        prefix_seen if masked else None,
                    )

            def suffix_step(step, inner):
                base = pl.multiple_of(step * suffix_chunk, suffix_chunk)

                def suffix_seen(shape):
                    key_row = base + lax.broadcasted_iota(jnp.int32, (shape[0], 1), 0)
                    return (
                        (key_row >= start)
                        & (key_row <= lane_row)
                        & (lane_row - key_row < window_len)
                    )

                absorb(suffix_ref[pl.ds(base, suffix_chunk), :], None, suffix_seen)
                return inner

            lax.fori_loop(
                start // suffix_chunk,
                (jnp.minimum(first_row + rows, end) - 1) // suffix_chunk + 1,
                suffix_step,
                0,
            )
            mine = (lane_row >= start) & (lane_row < end)
            result_scr[...] = jnp.where(mine, acc_scr[...] / total_scr[...], result_scr[...])

        return carry

    lax.fori_loop(0, requests, one_request, 0)
    for head in range(heads):
        out_ref[head * HD : (head + 1) * HD, :] = result_scr[
            :, head * rows : (head + 1) * rows
        ].astype(jnp.bfloat16)


def attention(scalars, queries, cosine, sine, windows, suffix, rows, piece, most_rows, window_len):
    width, own = queries.shape
    heads = width // HD
    member_count = len(windows)
    chunk = min(512, windows[0].shape[1])
    suffix_chunk = 256

    def whole(array):
        return pl.BlockSpec(array.shape, lambda t, s, n=array.ndim: (0,) * n)

    return pl.pallas_call(
        lambda *refs: attention_kernel(
            member_count, heads, piece, most_rows, window_len, chunk, suffix_chunk, *refs
        ),
        out_shape=jax.ShapeDtypeStruct((width, own), jnp.bfloat16),
        grid_spec=pltpu.PrefetchScalarGridSpec(
            num_scalar_prefetch=1,
            grid=(own // rows,),
            in_specs=[
                pl.BlockSpec((width, rows), lambda t, s: (0, t)),
                pl.BlockSpec((HD // 2, rows), lambda t, s: (0, t)),
                pl.BlockSpec((HD // 2, rows), lambda t, s: (0, t)),
                *[whole(window) for window in windows],
                whole(suffix),
            ],
            out_specs=pl.BlockSpec((width, rows), lambda t, s: (0, t)),
            scratch_shapes=[
                pltpu.VMEM((2 * HD, heads * rows), jnp.bfloat16),
                pltpu.VMEM((1, heads * rows), jnp.float32),
                pltpu.VMEM((1, heads * rows), jnp.float32),
                pltpu.VMEM((HD, heads * rows), jnp.float32),
                pltpu.VMEM((HD, heads * rows), jnp.float32),
            ],
        ),
        compiler_params=pltpu.CompilerParams(vmem_limit_bytes=48 * 2**20),
        cost_estimate=pl.CostEstimate(
            flops=20_000_000_000, bytes_accessed=8_000_000, transcendentals=10_000_000
        ),
        name="attention",
    )(scalars, queries, cosine, sine, *windows, suffix)


def shards(
    hidden_in,
    suffix_len,
    prefix_of,
    prefix_slot,
    prefix_cache,
    attn_gain,
    query_weight,
    keyval_weight,
    out_weight,
    mlp_gain,
    gate_weight,
    up_weight,
    down_weight,
    final_gain,
    head_weight,
):
    tok_count = lax.axis_size("tok")
    tok_place = lax.axis_index("tok")
    tok_rows = hidden_in.shape[0]
    own_rows = tok_rows * tok_count
    most_rows = own_rows // 2
    kv_count = keyval_weight.shape[0]
    members = tok_count // kv_count
    kv_head = tok_place // members
    member = tok_place % members
    alike = [[h * members + g for h in range(kv_count)] for g in range(members)]

    def shifted(array, shift):
        pairs = [
            (h * members + (g + shift) % members, h * members + g)
            for h in range(kv_count)
            for g in range(members)
        ]
        return lax.ppermute(array, "tok", pairs)

    lengths = suffix_len[0]
    starts, end_rows, offsets = owner_layout(lengths, own_rows)
    query_parts = [query_weight] + [shifted(query_weight, s) for s in range(1, members)]
    out_parts = [out_weight] + [shifted(out_weight, s) for s in range(1, members)]
    normed = rms_scale(hidden_in, attn_gain).astype(jnp.bfloat16)
    rows_here = lax.all_gather(normed, "tok", axis=0, tiled=True, axis_index_groups=alike)
    window_block = prefix_cache.shape[2]
    piece = window_block // members
    dealt = prefix_cache.reshape(1, tok_count, piece, 2 * HD)
    dealt = lax.all_to_all(dealt, "tok", split_axis=1, concat_axis=2, tiled=True)[:, 0]
    windows = [lax.all_gather(dealt, "req", axis=0, tiled=True)]
    windows += [shifted(windows[0], s) for s in range(1, members)]
    positions = lax.dynamic_index_in_dim(
        offsets.reshape(kv_count, members, tok_rows), member, 1, keepdims=False
    ).reshape(-1)
    positions = positions + PRE_LEN
    half = HD // 2
    levels = jnp.arange(half).astype(jnp.float32)
    inverse = jnp.exp(levels * (-2.0 * math.log(10000.0) / HD))
    angles = inverse[:, None] * positions.astype(jnp.float32)[None, :]
    cosine, sine = jnp.cos(angles), jnp.sin(angles)
    kv_weight = lax.dynamic_index_in_dim(keyval_weight, kv_head, 0, keepdims=False)
    keyvals = jnp.dot(rows_here, kv_weight, preferred_element_type=jnp.float32)
    low, high = keyvals[:, :half], keyvals[:, half:HD]
    cos_rows, sin_rows = cosine.T, sine.T
    keyvals = jnp.concatenate(
        [
            low * cos_rows - high * sin_rows,
            high * cos_rows + low * sin_rows,
            keyvals[:, HD:],
        ],
        axis=-1,
    ).astype(jnp.bfloat16)
    suffix = jnp.zeros((members, kv_count, tok_rows, 2 * HD), jnp.bfloat16)
    for s in range(members):
        part = keyvals if s == 0 else shifted(keyvals, s)
        suffix = lax.dynamic_update_index_in_dim(
            suffix, part.reshape(kv_count, tok_rows, 2 * HD), (member + s) % members, 0
        )
    suffix = jnp.transpose(suffix, (1, 0, 2, 3)).reshape(own_rows, 2 * HD)
    cache_width = kv_count * 2 * HD // tok_count
    cache_offset = tok_place * cache_width % (2 * HD)
    suffix_cache = lax.dynamic_slice_in_dim(suffix, cache_offset, cache_width, 1)
    queries = lax.dot_general(
        jnp.concatenate(query_parts, axis=1),
        rows_here,
        (((0,), (1,)), ((), ())),
        preferred_element_type=jnp.float32,
    )
    cache_rows = slot_lookup(prefix_of[0], prefix_slot)
    scalars = jnp.concatenate([starts, end_rows, cache_rows, member[None]]).astype(jnp.int32)
    attended = attention(
        scalars,
        queries,
        cosine,
        sine,
        windows,
        suffix,
        tok_rows,
        piece,
        most_rows,
        window_block * tok_count,
    )
    projected_back = lax.psum_scatter(
        lax.dot_general(
            attended,
            jnp.concatenate(out_parts, axis=0),
            (((0,), (0,)), ((), ())),
            preferred_element_type=jnp.float32,
        ).astype(jnp.bfloat16),
        "tok",
        scatter_dimension=0,
        tiled=True,
        axis_index_groups=alike,
    ).astype(jnp.float32)
    middle = (hidden_in.astype(jnp.float32) + projected_back).astype(jnp.bfloat16)
    mlp_in = rms_scale(middle, mlp_gain).astype(jnp.bfloat16)
    shard_part = lax.all_gather(mlp_in, "req", axis=0, tiled=True)
    gate_proj = jnp.dot(shard_part, gate_weight, preferred_element_type=jnp.float32)
    lifted = jnp.dot(shard_part, up_weight, preferred_element_type=jnp.float32)
    hidden_act = (jax.nn.silu(gate_proj) * lifted).astype(jnp.bfloat16)
    summed = lax.psum_scatter(
        jnp.dot(hidden_act, down_weight, preferred_element_type=jnp.float32).astype(jnp.bfloat16),
        "req",
        scatter_dimension=0,
        tiled=True,
    ).astype(jnp.float32)
    final_state = (middle.astype(jnp.float32) + summed).astype(jnp.bfloat16)
    local_index = jnp.arange(tok_rows) + tok_place * tok_rows
    picker = (local_index[None, :] == (end_rows - 1)[:, None]).astype(jnp.bfloat16)
    picked = jnp.dot(picker, final_state, preferred_element_type=jnp.float32)
    last_rows = lax.psum(picked.astype(jnp.bfloat16), "tok").astype(jnp.float32)
    mean_square = jnp.mean(last_rows * last_rows, axis=-1, keepdims=True)
    spread = jnp.sqrt(mean_square + epsilon)
    final_normed = (
        last_rows * lax.rsqrt(mean_square + epsilon) * final_gain.astype(jnp.float32)
    ).astype(jnp.bfloat16)
    logits = lax.dot_general(
        final_normed, head_weight, (((1,), (1,)), ((), ())), preferred_element_type=jnp.float32
    )
    local_high = jnp.max(logits, axis=-1)
    local_sum = jnp.sum(jnp.exp(logits - local_high[:, None]), axis=-1)
    pairs = lax.all_gather(jnp.stack([local_high, local_sum]), "tok", axis=0)
    highest = jnp.max(pairs[:, 0], axis=0)
    summed_exp = jnp.sum(pairs[:, 1] * jnp.exp(pairs[:, 0] - highest[None, :]), axis=0)
    log_total = highest + jnp.log(summed_exp)
    return (final_state, suffix_cache, spread[:, 0][None, :], highest[None, :], log_total[None, :])


def solution(mesh):
    placed = (
        P(("req", "tok"), None),
        P("req", None),
        P("req", None),
        P(),
        P("req", None, "tok", None),
        P(),
        P(None, "tok"),
        P(),
        P("tok", None),
        P(),
        P(None, "req"),
        P(None, "req"),
        P("req", None),
        P(),
        P("tok", None),
    )
    return jax.shard_map(
        shards,
        mesh=mesh,
        in_specs=placed,
        out_specs=(
            P(("req", "tok"), None),
            P("req", "tok"),
            P("req", None),
            P("req", None),
            P("req", None),
        ),
        check_vma=False,
    )
```

```python
import math

import jax
import jax.numpy as jnp
from jax import lax
from jax.experimental import pallas as pl
from jax.experimental.pallas import tpu as pltpu
from jax.sharding import PartitionSpec as P

HD = 64
PRE_LEN = 16384


epsilon = 1e-05
neg_large = -1e30


def rms_scale(values, gain_vec):
    widened = values.astype(jnp.float32)
    mean_square = jnp.mean(widened * widened, axis=-1, keepdims=True)
    return widened * lax.rsqrt(mean_square + epsilon) * gain_vec.astype(jnp.float32)


def owner_layout(lengths, row_count):
    end_rows = jnp.cumsum(lengths)
    starts = end_rows - lengths
    row_index = jnp.arange(row_count)
    member = (row_index[:, None] >= starts[None, :]) & (row_index[:, None] < end_rows[None, :])
    offsets = row_index - jnp.sum(jnp.where(member, starts[None, :], 0), axis=1)
    return (starts, end_rows, offsets)


def slot_lookup(chosen, prefix_slot):
    table_index = jnp.arange(prefix_slot.shape[0])
    hits = chosen[:, None] == table_index[None, :]
    return jnp.sum(jnp.where(hits, prefix_slot[None, :], 0), axis=1)


def attention_kernel(
    member_count,
    heads,
    piece,
    most_rows,
    window_len,
    chunk,
    suffix_chunk,
    scalars,
    q_ref,
    cos_ref,
    sin_ref,
    *refs,
):
    windows = refs[:member_count]
    suffix_ref, out_ref, query_scr, high_scr, total_scr, acc_scr, result_scr = refs[member_count:]
    requests = 4
    rows = q_ref.shape[1]
    half = HD // 2
    width = heads * rows
    member = scalars[3 * requests]
    tile = pl.program_id(0)
    first_row = (tile * member_count + member) * rows
    cosine = cos_ref[...]
    sine = sin_ref[...]
    for head in range(heads):
        low = q_ref[head * HD : head * HD + half, :]
        high = q_ref[head * HD + half : (head + 1) * HD, :]
        cols = pl.ds(head * rows, rows)
        turned = jnp.concatenate(
            [
                low * cosine - high * sine,
                high * cosine + low * sine,
                jnp.zeros((HD, rows), jnp.float32),
            ],
            axis=0,
        )
        query_scr[:, cols] = (turned * (HD**-0.5 * math.log2(math.e))).astype(jnp.bfloat16)

    def absorb(keyvals, row_of_key, visible_fn):
        scores = jnp.dot(keyvals, query_scr[...], preferred_element_type=jnp.float32)
        if visible_fn is not None:
            scores = jnp.where(visible_fn(scores.shape), scores, neg_large)
        before = high_scr[...]
        after = jnp.maximum(before, jnp.max(scores, axis=0, keepdims=True))
        weights = jnp.exp2(scores - after)
        fade = jnp.exp2(before - after)
        total_scr[...] = total_scr[...] * fade + jnp.sum(weights, axis=0, keepdims=True)
        mixed = lax.dot_general(
            keyvals,
            weights.astype(jnp.bfloat16),
            (((0,), (0,)), ((), ())),
            preferred_element_type=jnp.float32,
        )
        acc_scr[...] = acc_scr[...] * fade + mixed[HD:, :]
        high_scr[...] = after

    lane_row = first_row + lax.broadcasted_iota(jnp.int32, (1, width), 1) % rows

    def one_request(request, carry):
        start = scalars[request]
        end = scalars[requests + request]
        slot = scalars[2 * requests + request]

        @pl.when((start < first_row + rows) & (end > first_row))
        def _():
            high_scr[...] = jnp.full(high_scr.shape, neg_large, jnp.float32)
            total_scr[...] = jnp.zeros(total_scr.shape, jnp.float32)
            acc_scr[...] = jnp.zeros(acc_scr.shape, jnp.float32)
            offset = lane_row - start
            local_len = windows[0].shape[1]
            for first in reversed(range(0, local_len, chunk)):
                for shift in range(member_count):
                    part = lax.rem(member + shift, member_count)

                    def prefix_seen(shape, first=first, part=part):
                        index = first + lax.broadcasted_iota(jnp.int32, (shape[0], 1), 0)
                        position = (index // piece * member_count + part) * piece + index % piece
                        return position > offset

                    masked = first // piece * member_count * piece < most_rows
                    absorb(
                        windows[shift][slot, first : first + chunk, :],
                        None,
                        prefix_seen if masked else None,
                    )

            def suffix_step(step, inner):
                base = pl.multiple_of(step * suffix_chunk, suffix_chunk)

                def suffix_seen(shape):
                    key_row = base + lax.broadcasted_iota(jnp.int32, (shape[0], 1), 0)
                    return (
                        (key_row >= start)
                        & (key_row <= lane_row)
                        & (lane_row - key_row < window_len)
                    )

                absorb(suffix_ref[pl.ds(base, suffix_chunk), :], None, suffix_seen)
                return inner

            lax.fori_loop(
                start // suffix_chunk,
                (jnp.minimum(first_row + rows, end) - 1) // suffix_chunk + 1,
                suffix_step,
                0,
            )
            mine = (lane_row >= start) & (lane_row < end)
            result_scr[...] = jnp.where(mine, acc_scr[...] / total_scr[...], result_scr[...])

        return carry

    lax.fori_loop(0, requests, one_request, 0)
    for head in range(heads):
        out_ref[head * HD : (head + 1) * HD, :] = result_scr[
            :, head * rows : (head + 1) * rows
        ].astype(jnp.bfloat16)


def attention(scalars, queries, cosine, sine, windows, suffix, rows, piece, most_rows, window_len):
    width, own = queries.shape
    heads = width // HD
    member_count = len(windows)
    chunk = min(512, windows[0].shape[1])
    suffix_chunk = 256

    def whole(array):
        return pl.BlockSpec(array.shape, lambda t, s, n=array.ndim: (0,) * n)

    return pl.pallas_call(
        lambda *refs: attention_kernel(
            member_count, heads, piece, most_rows, window_len, chunk, suffix_chunk, *refs
        ),
        out_shape=jax.ShapeDtypeStruct((width, own), jnp.bfloat16),
        grid_spec=pltpu.PrefetchScalarGridSpec(
            num_scalar_prefetch=1,
            grid=(own // rows,),
            in_specs=[
                pl.BlockSpec((width, rows), lambda t, s: (0, t)),
                pl.BlockSpec((HD // 2, rows), lambda t, s: (0, t)),
                pl.BlockSpec((HD // 2, rows), lambda t, s: (0, t)),
                *[whole(window) for window in windows],
                whole(suffix),
            ],
            out_specs=pl.BlockSpec((width, rows), lambda t, s: (0, t)),
            scratch_shapes=[
                pltpu.VMEM((2 * HD, heads * rows), jnp.bfloat16),
                pltpu.VMEM((1, heads * rows), jnp.float32),
                pltpu.VMEM((1, heads * rows), jnp.float32),
                pltpu.VMEM((HD, heads * rows), jnp.float32),
                pltpu.VMEM((HD, heads * rows), jnp.float32),
            ],
        ),
        compiler_params=pltpu.CompilerParams(vmem_limit_bytes=48 * 2**20),
        cost_estimate=pl.CostEstimate(
            flops=20_000_000_000, bytes_accessed=8_000_000, transcendentals=10_000_000
        ),
        name="attention",
    )(scalars, queries, cosine, sine, *windows, suffix)


MESH = pl.DeviceIdType.MESH


def enter(groups):
    barrier = pltpu.get_barrier_semaphore()
    signals = 0
    for axis, count, stride in groups:
        place = lax.axis_index(axis)
        for shift in range(1, count):
            peer = lax.rem(place // stride + shift, count) * stride + lax.rem(place, stride)
            pl.semaphore_signal(barrier, inc=1, device_id={axis: peer}, device_id_type=MESH)
            signals += 1
    pl.semaphore_wait(barrier, signals)


def start_exchange(item, source, target, send, recv, local, row):
    scatter, (axis, count, stride) = item
    place = lax.axis_index(axis)
    mine = place // stride
    own = pltpu.make_async_copy(
        source.at[mine] if scatter else source, target.at[mine], local.at[row]
    )
    own.start()
    copies = [own]
    for shift in range(1, count):
        peer = lax.rem(mine + shift, count)
        copy = pltpu.make_async_remote_copy(
            src_ref=source.at[peer] if scatter else source,
            dst_ref=target.at[mine],
            send_sem=send.at[row, shift],
            recv_sem=recv.at[row, shift],
            device_id={axis: peer * stride + lax.rem(place, stride)},
            device_id_type=MESH,
        )
        copy.start()
        copies.append(copy)
    return copies


def remote_call(body, inputs, outputs, rows, most, collective_id, name):
    return pl.pallas_call(
        body,
        out_shape=outputs,
        in_specs=[pl.BlockSpec(memory_space=pl.ANY)] * len(inputs),
        out_specs=jax.tree.map(lambda _: pl.BlockSpec(memory_space=pl.ANY), outputs),
        scratch_shapes=[
            pltpu.SemaphoreType.DMA((rows, most)),
            pltpu.SemaphoreType.DMA((rows, most)),
            pltpu.SemaphoreType.DMA((rows,)),
        ],
        compiler_params=pltpu.CompilerParams(collective_id=collective_id, has_side_effects=True),
        name=name,
    )(*inputs)


def exchange(array, scatter, group, collective_id, name):
    def body(source, target, send, recv, local):
        enter([group])
        for copy in start_exchange((scatter, group), source, target, send, recv, local, 0):
            copy.wait()

    shape = array.shape if scatter else (group[1],) + array.shape
    return remote_call(
        body, [array], jax.ShapeDtypeStruct(shape, array.dtype), 1, group[1], collective_id, name
    )


def front_exchange(normed, dealt, alike, everyone, owners):
    def body(rows_ref, dealt_ref, all_rows, taken, windows, send, recv, local):
        enter([everyone, owners])
        first = start_exchange((True, everyone), dealt_ref, taken, send, recv, local, 0)
        second = start_exchange((False, alike), rows_ref, all_rows, send, recv, local, 1)
        for copy in first:
            copy.wait()
        third = start_exchange((False, owners), taken, windows, send, recv, local, 2)
        for copy in second + third:
            copy.wait()

    outputs = [
        jax.ShapeDtypeStruct((alike[1],) + normed.shape, normed.dtype),
        jax.ShapeDtypeStruct(dealt.shape, dealt.dtype),
        jax.ShapeDtypeStruct((owners[1],) + dealt.shape, dealt.dtype),
    ]
    most = max(alike[1], everyone[1], owners[1])
    return remote_call(body, [normed, dealt], outputs, 3, most, 0, "front_exchange")


def relay_gather(block, axis, count, collective_id, name):
    def body(source, target, send, recv, local):
        place = lax.axis_index(axis)
        has_left, has_right = place > 0, place < count - 1
        barrier = pltpu.get_barrier_semaphore()

        @pl.when(has_left)
        def _():
            pl.semaphore_signal(barrier, inc=1, device_id={axis: place - 1}, device_id_type=MESH)

        @pl.when(has_right)
        def _():
            pl.semaphore_signal(barrier, inc=1, device_id={axis: place + 1}, device_id_type=MESH)

        @pl.when(has_left & has_right)
        def _():
            pl.semaphore_wait(barrier, 2)

        @pl.when(jnp.logical_not(has_left & has_right))
        def _():
            pl.semaphore_wait(barrier, 1)

        own = pltpu.make_async_copy(source, target.at[place], local.at[0])
        own.start()

        def hop(step, toward):
            owner = lax.rem(place - toward * step + count, count)
            row = (1 - toward) // 2
            return pltpu.make_async_remote_copy(
                src_ref=source if step == 0 else target.at[owner],
                dst_ref=target.at[owner],
                send_sem=send.at[row, step],
                recv_sem=recv.at[row, step],
                device_id={axis: lax.rem(place + toward + count, count)},
                device_id_type=MESH,
            )

        def sends(step, toward):
            if toward == 1:
                return has_right & (place - step >= 0)
            return has_left & (place + step <= count - 1)

        def arrives(step, toward):
            if toward == 1:
                return place - 1 - step >= 0
            return place + 1 + step <= count - 1

        for step in range(count - 1):
            for toward in (1, -1):
                if step > 0:

                    @pl.when(arrives(step - 1, toward))
                    def _():
                        hop(step - 1, toward).wait_recv()

                @pl.when(sends(step, toward))
                def _():
                    hop(step, toward).start()

        for toward in (1, -1):

            @pl.when(arrives(count - 2, toward))
            def _():
                hop(count - 2, toward).wait_recv()

            for step in range(count - 1):

                @pl.when(sends(step, toward))
                def _():
                    hop(step, toward).wait_send()

        own.wait()

    return remote_call(
        body,
        [block],
        jax.ShapeDtypeStruct((count,) + block.shape, block.dtype),
        2,
        count,
        collective_id,
        name,
    )


def shards(
    hidden_in,
    suffix_len,
    prefix_of,
    prefix_slot,
    prefix_cache,
    attn_gain,
    query_weight,
    keyval_weight,
    out_weight,
    mlp_gain,
    gate_weight,
    up_weight,
    down_weight,
    final_gain,
    head_weight,
):
    tok_count = lax.axis_size("tok")
    tok_place = lax.axis_index("tok")
    tok_rows = hidden_in.shape[0]
    own_rows = tok_rows * tok_count
    most_rows = own_rows // 2
    kv_count = keyval_weight.shape[0]
    members = tok_count // kv_count
    kv_head = tok_place // members
    member = tok_place % members
    owner_count = lax.axis_size("req")
    alike = ("tok", kv_count, members)
    everyone = ("tok", tok_count, 1)
    owners = ("req", owner_count, 1)

    def shifted(array, shift):
        pairs = [
            (h * members + (g + shift) % members, h * members + g)
            for h in range(kv_count)
            for g in range(members)
        ]
        return lax.ppermute(array, "tok", pairs)

    lengths = suffix_len[0]
    starts, end_rows, offsets = owner_layout(lengths, own_rows)
    query_parts = [query_weight] + [shifted(query_weight, s) for s in range(1, members)]
    out_parts = [out_weight] + [shifted(out_weight, s) for s in range(1, members)]
    normed = rms_scale(hidden_in, attn_gain).astype(jnp.bfloat16)
    window_block = prefix_cache.shape[2]
    piece = window_block // members
    dealt = prefix_cache.reshape(tok_count, piece, 2 * HD)
    rows_here, unused, windows = front_exchange(normed, dealt, alike, everyone, owners)
    rows_here = rows_here.reshape(kv_count * tok_rows, -1)
    windows = [windows.reshape(owner_count, tok_count * piece, 2 * HD)]
    windows += [shifted(windows[0], s) for s in range(1, members)]
    positions = lax.dynamic_index_in_dim(
        offsets.reshape(kv_count, members, tok_rows), member, 1, keepdims=False
    ).reshape(-1)
    positions = positions + PRE_LEN
    half = HD // 2
    levels = jnp.arange(half).astype(jnp.float32)
    inverse = jnp.exp(levels * (-2.0 * math.log(10000.0) / HD))
    angles = inverse[:, None] * positions.astype(jnp.float32)[None, :]
    cosine, sine = jnp.cos(angles), jnp.sin(angles)
    kv_weight = lax.dynamic_index_in_dim(keyval_weight, kv_head, 0, keepdims=False)
    keyvals = jnp.dot(rows_here, kv_weight, preferred_element_type=jnp.float32)
    low, high = keyvals[:, :half], keyvals[:, half:HD]
    cos_rows, sin_rows = cosine.T, sine.T
    keyvals = jnp.concatenate(
        [
            low * cos_rows - high * sin_rows,
            high * cos_rows + low * sin_rows,
            keyvals[:, HD:],
        ],
        axis=-1,
    ).astype(jnp.bfloat16)
    suffix = jnp.zeros((members, kv_count, tok_rows, 2 * HD), jnp.bfloat16)
    for s in range(members):
        part = keyvals if s == 0 else shifted(keyvals, s)
        suffix = lax.dynamic_update_index_in_dim(
            suffix, part.reshape(kv_count, tok_rows, 2 * HD), (member + s) % members, 0
        )
    suffix = jnp.transpose(suffix, (1, 0, 2, 3)).reshape(own_rows, 2 * HD)
    cache_width = kv_count * 2 * HD // tok_count
    cache_offset = tok_place * cache_width % (2 * HD)
    suffix_cache = lax.dynamic_slice_in_dim(suffix, cache_offset, cache_width, 1)
    queries = lax.dot_general(
        jnp.concatenate(query_parts, axis=1),
        rows_here,
        (((0,), (1,)), ((), ())),
        preferred_element_type=jnp.float32,
    )
    cache_rows = slot_lookup(prefix_of[0], prefix_slot)
    scalars = jnp.concatenate([starts, end_rows, cache_rows, member[None]]).astype(jnp.int32)
    attended = attention(
        scalars,
        queries,
        cosine,
        sine,
        windows,
        suffix,
        tok_rows,
        piece,
        most_rows,
        window_block * tok_count,
    )
    partial = lax.dot_general(
        attended,
        jnp.concatenate(out_parts, axis=0),
        (((0,), (0,)), ((), ())),
        preferred_element_type=jnp.float32,
    ).astype(jnp.bfloat16)
    partial = exchange(partial.reshape(kv_count, tok_rows, -1), True, alike, 1, "out_exchange")
    projected_back = jnp.sum(partial.astype(jnp.float32), axis=0)
    middle = (hidden_in.astype(jnp.float32) + projected_back).astype(jnp.bfloat16)
    mlp_in = rms_scale(middle, mlp_gain).astype(jnp.bfloat16)
    shard_part = relay_gather(mlp_in, "req", owner_count, 2, "mlp_gather")
    shard_part = shard_part.reshape(owner_count * tok_rows, -1)
    gate_proj = jnp.dot(shard_part, gate_weight, preferred_element_type=jnp.float32)
    lifted = jnp.dot(shard_part, up_weight, preferred_element_type=jnp.float32)
    hidden_act = (jax.nn.silu(gate_proj) * lifted).astype(jnp.bfloat16)
    summed = lax.psum_scatter(
        jnp.dot(hidden_act, down_weight, preferred_element_type=jnp.float32).astype(jnp.bfloat16),
        "req",
        scatter_dimension=0,
        tiled=True,
    ).astype(jnp.float32)
    final_state = (middle.astype(jnp.float32) + summed).astype(jnp.bfloat16)
    local_index = jnp.arange(tok_rows) + tok_place * tok_rows
    picker = (local_index[None, :] == (end_rows - 1)[:, None]).astype(jnp.bfloat16)
    picked = jnp.dot(picker, final_state, preferred_element_type=jnp.float32)
    picked = exchange(picked.astype(jnp.bfloat16), False, everyone, 3, "last_exchange")
    last_rows = jnp.sum(picked.astype(jnp.float32), axis=0)
    mean_square = jnp.mean(last_rows * last_rows, axis=-1, keepdims=True)
    spread = jnp.sqrt(mean_square + epsilon)
    final_normed = (
        last_rows * lax.rsqrt(mean_square + epsilon) * final_gain.astype(jnp.float32)
    ).astype(jnp.bfloat16)
    logits = lax.dot_general(
        final_normed, head_weight, (((1,), (1,)), ((), ())), preferred_element_type=jnp.float32
    )
    local_high = jnp.max(logits, axis=-1)
    local_sum = jnp.sum(jnp.exp(logits - local_high[:, None]), axis=-1)
    pairs = jnp.pad(jnp.stack([local_high, local_sum]), ((0, 6), (0, 128 - starts.shape[0])))
    pairs = exchange(pairs, False, everyone, 4, "tail_exchange")[:, :, : starts.shape[0]]
    highest = jnp.max(pairs[:, 0], axis=0)
    summed_exp = jnp.sum(pairs[:, 1] * jnp.exp(pairs[:, 0] - highest[None, :]), axis=0)
    log_total = highest + jnp.log(summed_exp)
    return (final_state, suffix_cache, spread[:, 0][None, :], highest[None, :], log_total[None, :])


def solution(mesh):
    placed = (
        P(("req", "tok"), None),
        P("req", None),
        P("req", None),
        P(),
        P("req", None, "tok", None),
        P(),
        P(None, "tok"),
        P(),
        P("tok", None),
        P(),
        P(None, "req"),
        P(None, "req"),
        P("req", None),
        P(),
        P("tok", None),
    )
    return jax.shard_map(
        shards,
        mesh=mesh,
        in_specs=placed,
        out_specs=(
            P(("req", "tok"), None),
            P("req", "tok"),
            P("req", None),
            P("req", None),
            P("req", None),
        ),
        check_vma=False,
    )
```

```python
import math

import jax
import jax.numpy as jnp
from jax import lax
from jax.experimental import pallas as pl
from jax.experimental.pallas import tpu as pltpu
from jax.sharding import PartitionSpec as P

HD = 64
PRE_LEN = 16384


epsilon = 1e-05
neg_large = -1e30


def rms_scale(values, gain_vec):
    widened = values.astype(jnp.float32)
    mean_square = jnp.mean(widened * widened, axis=-1, keepdims=True)
    return widened * lax.rsqrt(mean_square + epsilon) * gain_vec.astype(jnp.float32)


def owner_layout(lengths, row_count):
    end_rows = jnp.cumsum(lengths)
    starts = end_rows - lengths
    row_index = jnp.arange(row_count)
    member = (row_index[:, None] >= starts[None, :]) & (row_index[:, None] < end_rows[None, :])
    offsets = row_index - jnp.sum(jnp.where(member, starts[None, :], 0), axis=1)
    return (starts, end_rows, offsets)


def slot_lookup(chosen, prefix_slot):
    table_index = jnp.arange(prefix_slot.shape[0])
    hits = chosen[:, None] == table_index[None, :]
    return jnp.sum(jnp.where(hits, prefix_slot[None, :], 0), axis=1)


def attention_kernel(
    member_count,
    heads,
    piece,
    most_rows,
    window_len,
    chunk,
    suffix_chunk,
    scalars,
    q_ref,
    cos_ref,
    sin_ref,
    *refs,
):
    windows = refs[:member_count]
    suffix_ref, out_ref, query_scr, high_scr, total_scr, acc_scr, result_scr = refs[member_count:]
    requests = 4
    rows = q_ref.shape[1]
    half = HD // 2
    width = heads * rows
    member = scalars[3 * requests]
    tile = pl.program_id(0)
    first_row = (tile * member_count + member) * rows
    cosine = cos_ref[...]
    sine = sin_ref[...]
    for head in range(heads):
        low = q_ref[head * HD : head * HD + half, :]
        high = q_ref[head * HD + half : (head + 1) * HD, :]
        cols = pl.ds(head * rows, rows)
        turned = jnp.concatenate(
            [
                low * cosine - high * sine,
                high * cosine + low * sine,
                jnp.zeros((HD, rows), jnp.float32),
            ],
            axis=0,
        )
        query_scr[:, cols] = (turned * (HD**-0.5 * math.log2(math.e))).astype(jnp.bfloat16)

    def absorb(keyvals, row_of_key, visible_fn):
        scores = jnp.dot(keyvals, query_scr[...], preferred_element_type=jnp.float32)
        if visible_fn is not None:
            scores = jnp.where(visible_fn(scores.shape), scores, neg_large)
        before = high_scr[...]
        after = jnp.maximum(before, jnp.max(scores, axis=0, keepdims=True))
        weights = jnp.exp2(scores - after)
        fade = jnp.exp2(before - after)
        total_scr[...] = total_scr[...] * fade + jnp.sum(weights, axis=0, keepdims=True)
        mixed = lax.dot_general(
            keyvals,
            weights.astype(jnp.bfloat16),
            (((0,), (0,)), ((), ())),
            preferred_element_type=jnp.float32,
        )
        acc_scr[...] = acc_scr[...] * fade + mixed[HD:, :]
        high_scr[...] = after

    lane_row = first_row + lax.broadcasted_iota(jnp.int32, (1, width), 1) % rows

    def one_request(request, carry):
        start = scalars[request]
        end = scalars[requests + request]
        slot = scalars[2 * requests + request]

        @pl.when((start < first_row + rows) & (end > first_row))
        def _():
            high_scr[...] = jnp.full(high_scr.shape, neg_large, jnp.float32)
            total_scr[...] = jnp.zeros(total_scr.shape, jnp.float32)
            acc_scr[...] = jnp.zeros(acc_scr.shape, jnp.float32)
            offset = lane_row - start
            local_len = windows[0].shape[1]
            for first in reversed(range(0, local_len, chunk)):
                for shift in range(member_count):
                    part = lax.rem(member + shift, member_count)

                    def prefix_seen(shape, first=first, part=part):
                        index = first + lax.broadcasted_iota(jnp.int32, (shape[0], 1), 0)
                        position = (index // piece * member_count + part) * piece + index % piece
                        return position > offset

                    masked = first // piece * member_count * piece < most_rows
                    absorb(
                        windows[shift][slot, first : first + chunk, :],
                        None,
                        prefix_seen if masked else None,
                    )

            def suffix_step(step, inner):
                base = pl.multiple_of(step * suffix_chunk, suffix_chunk)

                def suffix_seen(shape):
                    key_row = base + lax.broadcasted_iota(jnp.int32, (shape[0], 1), 0)
                    return (
                        (key_row >= start)
                        & (key_row <= lane_row)
                        & (lane_row - key_row < window_len)
                    )

                absorb(suffix_ref[pl.ds(base, suffix_chunk), :], None, suffix_seen)
                return inner

            lax.fori_loop(
                start // suffix_chunk,
                (jnp.minimum(first_row + rows, end) - 1) // suffix_chunk + 1,
                suffix_step,
                0,
            )
            mine = (lane_row >= start) & (lane_row < end)
            result_scr[...] = jnp.where(mine, acc_scr[...] / total_scr[...], result_scr[...])

        return carry

    lax.fori_loop(0, requests, one_request, 0)
    for head in range(heads):
        out_ref[head * HD : (head + 1) * HD, :] = result_scr[
            :, head * rows : (head + 1) * rows
        ].astype(jnp.bfloat16)


def attention(scalars, queries, cosine, sine, windows, suffix, rows, piece, most_rows, window_len):
    width, own = queries.shape
    heads = width // HD
    member_count = len(windows)
    chunk = min(512, windows[0].shape[1])
    suffix_chunk = 256

    def whole(array):
        return pl.BlockSpec(array.shape, lambda t, s, n=array.ndim: (0,) * n)

    return pl.pallas_call(
        lambda *refs: attention_kernel(
            member_count, heads, piece, most_rows, window_len, chunk, suffix_chunk, *refs
        ),
        out_shape=jax.ShapeDtypeStruct((width, own), jnp.bfloat16),
        grid_spec=pltpu.PrefetchScalarGridSpec(
            num_scalar_prefetch=1,
            grid=(own // rows,),
            in_specs=[
                pl.BlockSpec((width, rows), lambda t, s: (0, t)),
                pl.BlockSpec((HD // 2, rows), lambda t, s: (0, t)),
                pl.BlockSpec((HD // 2, rows), lambda t, s: (0, t)),
                *[whole(window) for window in windows],
                whole(suffix),
            ],
            out_specs=pl.BlockSpec((width, rows), lambda t, s: (0, t)),
            scratch_shapes=[
                pltpu.VMEM((2 * HD, heads * rows), jnp.bfloat16),
                pltpu.VMEM((1, heads * rows), jnp.float32),
                pltpu.VMEM((1, heads * rows), jnp.float32),
                pltpu.VMEM((HD, heads * rows), jnp.float32),
                pltpu.VMEM((HD, heads * rows), jnp.float32),
            ],
        ),
        compiler_params=pltpu.CompilerParams(vmem_limit_bytes=48 * 2**20),
        cost_estimate=pl.CostEstimate(
            flops=20_000_000_000, bytes_accessed=8_000_000, transcendentals=10_000_000
        ),
        name="attention",
    )(scalars, queries, cosine, sine, *windows, suffix)


MESH = pl.DeviceIdType.MESH


def enter(groups):
    barrier = pltpu.get_barrier_semaphore()
    signals = 0
    for axis, count, stride in groups:
        place = lax.axis_index(axis)
        for shift in range(1, count):
            peer = lax.rem(place // stride + shift, count) * stride + lax.rem(place, stride)
            pl.semaphore_signal(barrier, inc=1, device_id={axis: peer}, device_id_type=MESH)
            signals += 1
    pl.semaphore_wait(barrier, signals)


def start_exchange(item, source, target, send, recv, local, row):
    scatter, (axis, count, stride) = item
    place = lax.axis_index(axis)
    mine = place // stride
    own = pltpu.make_async_copy(
        source.at[mine] if scatter else source, target.at[mine], local.at[row]
    )
    own.start()
    copies = [own]
    for shift in range(1, count):
        peer = lax.rem(mine + shift, count)
        copy = pltpu.make_async_remote_copy(
            src_ref=source.at[peer] if scatter else source,
            dst_ref=target.at[mine],
            send_sem=send.at[row, shift],
            recv_sem=recv.at[row, shift],
            device_id={axis: peer * stride + lax.rem(place, stride)},
            device_id_type=MESH,
        )
        copy.start()
        copies.append(copy)
    return copies


def remote_call(body, inputs, outputs, rows, most, collective_id, name):
    return pl.pallas_call(
        body,
        out_shape=outputs,
        in_specs=[pl.BlockSpec(memory_space=pl.ANY)] * len(inputs),
        out_specs=jax.tree.map(lambda _: pl.BlockSpec(memory_space=pl.ANY), outputs),
        scratch_shapes=[
            pltpu.SemaphoreType.DMA((rows, most)),
            pltpu.SemaphoreType.DMA((rows, most)),
            pltpu.SemaphoreType.DMA((rows,)),
        ],
        compiler_params=pltpu.CompilerParams(collective_id=collective_id, has_side_effects=True),
        name=name,
    )(*inputs)


def exchange(array, scatter, group, collective_id, name):
    def body(source, target, send, recv, local):
        enter([group])
        for copy in start_exchange((scatter, group), source, target, send, recv, local, 0):
            copy.wait()

    shape = array.shape if scatter else (group[1],) + array.shape
    return remote_call(
        body, [array], jax.ShapeDtypeStruct(shape, array.dtype), 1, group[1], collective_id, name
    )


def front_exchange(normed, dealt, alike, everyone, owners):
    def body(rows_ref, dealt_ref, all_rows, taken, windows, send, recv, local):
        enter([everyone, owners])
        first = start_exchange((True, everyone), dealt_ref, taken, send, recv, local, 0)
        second = start_exchange((False, alike), rows_ref, all_rows, send, recv, local, 1)
        for copy in first:
            copy.wait()
        third = start_exchange((False, owners), taken, windows, send, recv, local, 2)
        for copy in second + third:
            copy.wait()

    outputs = [
        jax.ShapeDtypeStruct((alike[1],) + normed.shape, normed.dtype),
        jax.ShapeDtypeStruct(dealt.shape, dealt.dtype),
        jax.ShapeDtypeStruct((owners[1],) + dealt.shape, dealt.dtype),
    ]
    most = max(alike[1], everyone[1], owners[1])
    return remote_call(body, [normed, dealt], outputs, 3, most, 0, "front_exchange")


def relay_gather(block, axis, count, collective_id, name):
    def body(source, target, send, recv, local):
        place = lax.axis_index(axis)
        has_left, has_right = place > 0, place < count - 1
        barrier = pltpu.get_barrier_semaphore()

        @pl.when(has_left)
        def _():
            pl.semaphore_signal(barrier, inc=1, device_id={axis: place - 1}, device_id_type=MESH)

        @pl.when(has_right)
        def _():
            pl.semaphore_signal(barrier, inc=1, device_id={axis: place + 1}, device_id_type=MESH)

        @pl.when(has_left & has_right)
        def _():
            pl.semaphore_wait(barrier, 2)

        @pl.when(jnp.logical_not(has_left & has_right))
        def _():
            pl.semaphore_wait(barrier, 1)

        own = pltpu.make_async_copy(source, target.at[place], local.at[0])
        own.start()

        def hop(step, toward):
            owner = lax.rem(place - toward * step + count, count)
            row = (1 - toward) // 2
            return pltpu.make_async_remote_copy(
                src_ref=source if step == 0 else target.at[owner],
                dst_ref=target.at[owner],
                send_sem=send.at[row, step],
                recv_sem=recv.at[row, step],
                device_id={axis: lax.rem(place + toward + count, count)},
                device_id_type=MESH,
            )

        def sends(step, toward):
            if toward == 1:
                return has_right & (place - step >= 0)
            return has_left & (place + step <= count - 1)

        def arrives(step, toward):
            if toward == 1:
                return place - 1 - step >= 0
            return place + 1 + step <= count - 1

        for step in range(count - 1):
            for toward in (1, -1):
                if step > 0:

                    @pl.when(arrives(step - 1, toward))
                    def _():
                        hop(step - 1, toward).wait_recv()

                @pl.when(sends(step, toward))
                def _():
                    hop(step, toward).start()

        for toward in (1, -1):

            @pl.when(arrives(count - 2, toward))
            def _():
                hop(count - 2, toward).wait_recv()

            for step in range(count - 1):

                @pl.when(sends(step, toward))
                def _():
                    hop(step, toward).wait_send()

        own.wait()

    return remote_call(
        body,
        [block],
        jax.ShapeDtypeStruct((count,) + block.shape, block.dtype),
        2,
        count,
        collective_id,
        name,
    )


def shards(
    hidden_in,
    suffix_len,
    prefix_of,
    prefix_slot,
    prefix_cache,
    attn_gain,
    query_weight,
    keyval_weight,
    out_weight,
    mlp_gain,
    gate_weight,
    up_weight,
    down_weight,
    final_gain,
    head_weight,
):
    tok_count = lax.axis_size("tok")
    tok_place = lax.axis_index("tok")
    tok_rows = hidden_in.shape[0]
    own_rows = tok_rows * tok_count
    most_rows = own_rows // 2
    kv_count = keyval_weight.shape[0]
    members = tok_count // kv_count
    kv_head = tok_place // members
    member = tok_place % members
    owner_count = lax.axis_size("req")
    alike = ("tok", kv_count, members)
    everyone = ("tok", tok_count, 1)
    owners = ("req", owner_count, 1)

    def shifted(array, shift):
        pairs = [
            (h * members + (g + shift) % members, h * members + g)
            for h in range(kv_count)
            for g in range(members)
        ]
        return lax.ppermute(array, "tok", pairs)

    lengths = suffix_len[0]
    starts, end_rows, offsets = owner_layout(lengths, own_rows)
    query_parts = [query_weight] + [shifted(query_weight, s) for s in range(1, members)]
    out_parts = [out_weight] + [shifted(out_weight, s) for s in range(1, members)]
    normed = rms_scale(hidden_in, attn_gain).astype(jnp.bfloat16)
    window_block = prefix_cache.shape[2]
    piece = window_block // members
    dealt = prefix_cache.reshape(tok_count, piece, 2 * HD)
    rows_here, unused, windows = front_exchange(normed, dealt, alike, everyone, owners)
    rows_here = rows_here.reshape(kv_count * tok_rows, -1)
    windows = [windows.reshape(owner_count, tok_count * piece, 2 * HD)]
    windows += [shifted(windows[0], s) for s in range(1, members)]
    positions = lax.dynamic_index_in_dim(
        offsets.reshape(kv_count, members, tok_rows), member, 1, keepdims=False
    ).reshape(-1)
    positions = positions + PRE_LEN
    half = HD // 2
    levels = jnp.arange(half).astype(jnp.float32)
    inverse = jnp.exp(levels * (-2.0 * math.log(10000.0) / HD))
    angles = inverse[:, None] * positions.astype(jnp.float32)[None, :]
    cosine, sine = jnp.cos(angles), jnp.sin(angles)
    kv_weight = lax.dynamic_index_in_dim(keyval_weight, kv_head, 0, keepdims=False)
    keyvals = jnp.dot(rows_here, kv_weight, preferred_element_type=jnp.float32)
    low, high = keyvals[:, :half], keyvals[:, half:HD]
    cos_rows, sin_rows = cosine.T, sine.T
    keyvals = jnp.concatenate(
        [
            low * cos_rows - high * sin_rows,
            high * cos_rows + low * sin_rows,
            keyvals[:, HD:],
        ],
        axis=-1,
    ).astype(jnp.bfloat16)
    suffix = jnp.zeros((members, kv_count, tok_rows, 2 * HD), jnp.bfloat16)
    for s in range(members):
        part = keyvals if s == 0 else shifted(keyvals, s)
        suffix = lax.dynamic_update_index_in_dim(
            suffix, part.reshape(kv_count, tok_rows, 2 * HD), (member + s) % members, 0
        )
    suffix = jnp.transpose(suffix, (1, 0, 2, 3)).reshape(own_rows, 2 * HD)
    cache_width = kv_count * 2 * HD // tok_count
    cache_offset = tok_place * cache_width % (2 * HD)
    suffix_cache = lax.dynamic_slice_in_dim(suffix, cache_offset, cache_width, 1)
    queries = lax.dot_general(
        jnp.concatenate(query_parts, axis=1),
        rows_here,
        (((0,), (1,)), ((), ())),
        preferred_element_type=jnp.float32,
    )
    cache_rows = slot_lookup(prefix_of[0], prefix_slot)
    scalars = jnp.concatenate([starts, end_rows, cache_rows, member[None]]).astype(jnp.int32)
    attended = attention(
        scalars,
        queries,
        cosine,
        sine,
        windows,
        suffix,
        tok_rows,
        piece,
        most_rows,
        window_block * tok_count,
    )
    partial = lax.dot_general(
        attended,
        jnp.concatenate(out_parts, axis=0),
        (((0,), (0,)), ((), ())),
        preferred_element_type=jnp.float32,
    ).astype(jnp.bfloat16)
    partial = exchange(partial.reshape(kv_count, tok_rows, -1), True, alike, 1, "out_exchange")
    projected_back = jnp.sum(partial.astype(jnp.float32), axis=0)
    middle = (hidden_in.astype(jnp.float32) + projected_back).astype(jnp.bfloat16)
    mlp_in = rms_scale(middle, mlp_gain).astype(jnp.bfloat16)
    shard_part = relay_gather(mlp_in, "req", owner_count, 2, "mlp_gather")
    shard_part = shard_part.reshape(owner_count * tok_rows, -1)
    gate_proj = jnp.dot(shard_part, gate_weight, preferred_element_type=jnp.float32)
    lifted = jnp.dot(shard_part, up_weight, preferred_element_type=jnp.float32)
    hidden_act = (jax.nn.silu(gate_proj) * lifted).astype(jnp.bfloat16)
    shares = jnp.dot(hidden_act, down_weight, preferred_element_type=jnp.float32)
    shares = shares.astype(jnp.bfloat16).reshape(owner_count, tok_rows, -1)
    shares = exchange(shares, True, owners, 5, "mlp_exchange")
    summed = jnp.sum(shares.astype(jnp.float32), axis=0)
    final_state = (middle.astype(jnp.float32) + summed).astype(jnp.bfloat16)
    local_index = jnp.arange(tok_rows) + tok_place * tok_rows
    picker = (local_index[None, :] == (end_rows - 1)[:, None]).astype(jnp.bfloat16)
    picked = jnp.dot(picker, final_state, preferred_element_type=jnp.float32)
    picked = exchange(picked.astype(jnp.bfloat16), False, everyone, 3, "last_exchange")
    last_rows = jnp.sum(picked.astype(jnp.float32), axis=0)
    mean_square = jnp.mean(last_rows * last_rows, axis=-1, keepdims=True)
    spread = jnp.sqrt(mean_square + epsilon)
    final_normed = (
        last_rows * lax.rsqrt(mean_square + epsilon) * final_gain.astype(jnp.float32)
    ).astype(jnp.bfloat16)
    logits = lax.dot_general(
        final_normed, head_weight, (((1,), (1,)), ((), ())), preferred_element_type=jnp.float32
    )
    local_high = jnp.max(logits, axis=-1)
    local_sum = jnp.sum(jnp.exp(logits - local_high[:, None]), axis=-1)
    pairs = jnp.pad(jnp.stack([local_high, local_sum]), ((0, 6), (0, 128 - starts.shape[0])))
    pairs = exchange(pairs, False, everyone, 4, "tail_exchange")[:, :, : starts.shape[0]]
    highest = jnp.max(pairs[:, 0], axis=0)
    summed_exp = jnp.sum(pairs[:, 1] * jnp.exp(pairs[:, 0] - highest[None, :]), axis=0)
    log_total = highest + jnp.log(summed_exp)
    return (final_state, suffix_cache, spread[:, 0][None, :], highest[None, :], log_total[None, :])


def solution(mesh):
    placed = (
        P(("req", "tok"), None),
        P("req", None),
        P("req", None),
        P(),
        P("req", None, "tok", None),
        P(),
        P(None, "tok"),
        P(),
        P("tok", None),
        P(),
        P(None, "req"),
        P(None, "req"),
        P("req", None),
        P(),
        P("tok", None),
    )
    return jax.shard_map(
        shards,
        mesh=mesh,
        in_specs=placed,
        out_specs=(
            P(("req", "tok"), None),
            P("req", "tok"),
            P("req", None),
            P("req", None),
            P("req", None),
        ),
        check_vma=False,
    )
```
